256 devices in a mesh: row: 8 (over x, z_hi), col: 8 (over z_lo, core), layer: 4 (over y).
Axes of the slice: x: 4, y: 4, z: 8 (z_hi: 2, z_lo: 4; z = z_hi * 4 + z_lo), core: 2. Of those that a mesh axis runs over, the one named last changes fastest.
Arguments:
- amplitudes: float32 [4096, 2048], P('row', ('col', 'layer')), may hold values from -6 to 6
- integrals: float32 [2048, 16384], P(('row', 'layer'), 'col'), may hold values from -0.125 to 0.125
Outputs:
- ladder: float32 [4096, 16384], P('row', ('col', 'layer'))
The draws below stay inside these ranges and needn't reach their ends.
All inputs are finite; a program needn't handle non-finite values.
Results may differ from the reference program's by a relative error of at most 0.000082.
Values sent between devices are 32-bit elements; how exact they have to be, the bound alone decides.
A program may use at most 64 MiB of HBM per device.

```python
import jax
import jax.numpy as jnp
from jax import lax

CONTR = 2048
OUTW = 16384
ROWS = 4096


def block_scale(rng, extent, pieces, low, largest):
    level = 1.0
    for axis_at, blocks in pieces:
        steps = jax.random.uniform(jax.random.fold_in(jax.random.fold_in(rng, 6), axis_at), (blocks,), jnp.float32, low / len(pieces), largest / len(pieces))
        level = level * jnp.repeat(jnp.exp(steps), extent[axis_at] // blocks).reshape((-1,) + (1,) * (len(extent) - 1 - axis_at))
    return level


def centred(stream_key, shape, width, bound, cuts=(), dtype=jnp.bfloat16):
    gain = block_scale(stream_key, shape, cuts, -0.22, 0.18) if cuts else 1.0
    values = jax.random.normal(stream_key, shape, jnp.float32) * width * gain
    return jnp.minimum(jnp.maximum(values, -bound), bound).astype(dtype)


def setup_inputs(seed: int = 0) -> dict:
    key_list = jax.random.split(jax.random.key(seed), 3)
    amplitudes = centred(key_list[0], (ROWS, CONTR), 1.0, 6.0, ((0, 8), (1, 32)), jnp.float32)
    integrals = centred(key_list[1], (CONTR, OUTW), CONTR ** -0.5, 0.125, ((0, 32), (1, 8)), jnp.float32)
    return {"amplitudes": amplitudes, "integrals": integrals}


def reference(amplitudes, integrals):
    product = jnp.dot(amplitudes, integrals, precision=lax.Precision.HIGHEST, preferred_element_type=jnp.float32)
    return 0.5 * product
```

```python
import jax
import jax.numpy as jnp
from jax import lax
from jax.experimental import pallas as pl
from jax.experimental.pallas import tpu as pltpu
from jax.sharding import PartitionSpec as P

MESH = pl.DeviceIdType.MESH
F32, BF16 = jnp.float32, jnp.bfloat16
STEPS = (0, -1, 1, 2)


def split(v):
    hi = v.astype(BF16)
    return hi, (v - hi.astype(F32)).astype(BF16)


def kernel(
    a_ref, b_ref, o_ref, abuf, bbuf, acat, bcat,
    local_sem, a_recv, b_recv, a_send, b_send, y_send, relay_send,
):
    row, col, y = lax.axis_index("row"), lax.axis_index("col"), lax.axis_index("layer")
    x, zh, zl, q = row // 2, row % 2, col // 2, col % 2
    z = zh * 4 + zl

    def device(x_at, y_at, z_at, q_at):
        x_at, y_at, z_at = (x_at + 4) % 4, (y_at + 4) % 4, (z_at + 8) % 8
        return (x_at * 2 + z_at // 4, (z_at % 4) * 2 + q_at, y_at)

    right_x, left_x = device(x + 1, y, z, q), device(x - 1, y, z, q)
    over_z = device(x, y, z + 4, q)
    up_z, down_z = device(x, y, z + 1, q), device(x, y, z - 1, q)
    partner = device(x, y, z, 1 - q)
    y_to = [device(x, y + d, z, q) for d in (1, -1, 2)]

    def at_y(d):
        return (y + d + 4) % 4

    def at_x(d):
        return (x + d + 4) % 4

    def remote(src, dst, send, recv, to):
        return pltpu.make_async_remote_copy(
            src_ref=src, dst_ref=dst, send_sem=send, recv_sem=recv, device_id=to, device_id_type=MESH
        )

    def b_cols(y_at):
        return b_ref.at[:, pl.ds(pl.multiple_of(y_at * 512, 512), 512)]

    sent = []

    def go(copy, cond=None):
        if cond is None:
            copy.start()
        else:
            pl.when(cond)(copy.start)
        sent.append((copy, cond))

    def b_wait(h, y_at, x_at, part=None):
        dst = bbuf.at[h, y_at, x_at] if part is None else bbuf.at[h, y_at, x_at, pl.ds(part * 32, 32)]
        sem = b_recv.at[h, y_at, x_at, 0 if part is None else part]
        pltpu.make_async_copy(dst, dst, sem).wait()

    def b_spread(h, y_at, src, over):
        dst, recv = bbuf.at[h, y_at, x], b_recv.at[h, y_at, x, 0]
        go(remote(src, dst, b_send.at[h, y_at, 0], recv, right_x))
        go(remote(src, dst, b_send.at[h, y_at, 1], recv, left_x))
        if over:
            go(remote(src, dst, b_send.at[h, y_at, 2], recv, over_z))

    def b_own(k, h, over):
        y_at = at_y(STEPS[k])
        b_wait(h, y_at, x)
        b_spread(h, y_at, bbuf.at[h, y_at, x], over)

    def b_relay(k, h):
        y_at = at_y(STEPS[k])
        for part, (d, to) in enumerate(((-1, right_x), (1, left_x))):
            x_at = at_x(d)
            b_wait(h, y_at, x_at)
            half = bbuf.at[h, y_at, x_at, pl.ds(part * 32, 32)]
            go(remote(half, half, relay_send.at[h, y_at, part], b_recv.at[h, y_at, x_at, part], to))

    def a_wait(q_at, y_at, zl_at):
        dst = abuf.at[q_at, y_at, zl_at]
        pltpu.make_async_copy(dst, dst, a_recv.at[q_at, y_at, zl_at]).wait()

    def a_copy(y_at, zl_at, i, to, own=False):
        blk = abuf.at[q, y_at, zl_at]
        return remote(a_ref if own else blk, blk, a_send.at[y_at, zl_at, i], a_recv.at[q, y_at, zl_at], to)

    def both(*conds):
        out = None
        for c in conds:
            if c is not None:
                out = c if out is None else jnp.logical_and(out, c)
        return out

    slots = [(0, None, 0)]
    for s in (1, 2, 3):
        slots += [(-s, zl >= s, 1), (s, zl + s <= 3, -1)]

    def a_slot(i):
        d, cond, way = slots[i]
        zl_at = jnp.clip(zl + d, 0, 3)
        if way != 0:
            pl.when(cond)(lambda: a_wait(q, y, zl_at))
        if way >= 0:
            go(a_copy(y, zl_at, 0, up_z, way == 0), both(cond, zl <= 2))
        if way <= 0:
            go(a_copy(y, zl_at, 1, down_z, way == 0), both(cond, zl >= 1))
        for n in range(3):
            go(a_copy(y, zl_at, 2 + n, y_to[n], way == 0), cond)
        go(a_copy(y, zl_at, 5, partner, way == 0), cond)

    def a_from_y(i):
        d, cond, _ = slots[i]
        zl_at = jnp.clip(zl + d, 0, 3)
        for dy in (-1, 1, 2):
            y_at = at_y(dy)
            if cond is None:
                a_wait(q, y_at, zl_at)
            else:
                pl.when(cond)(lambda: a_wait(q, y_at, zl_at))
            go(a_copy(y_at, zl_at, 5, partner), cond)

    def a_partner(y_at):
        for zl_at in range(4):
            a_wait(1 - q, y_at, zl_at)

    def compute(k, h, first=False):
        y_at = at_y(STEPS[k])
        for i in range(4):
            for rows in range(0, 512, 128):
                if i % 2 == 0:
                    v = jnp.concatenate([abuf[h, y_at, i, :, rows:rows + 128], abuf[h, y_at, i + 1, :, rows:rows + 128]], axis=0)
                    hi, lo = split(v.T)
                    cols = i * 64
                    acat[rows:rows + 128, cols:cols + 128] = hi
                    acat[rows:rows + 128, 256 + cols:256 + cols + 128] = hi
                    acat[rows:rows + 128, 512 + cols:512 + cols + 128] = lo
        for i in range(4):
            hi, lo = split(bbuf[h, y_at, i])
            bcat[i * 64:i * 64 + 64] = hi
            bcat[256 + i * 64:256 + i * 64 + 64] = lo
            bcat[512 + i * 64:512 + i * 64 + 64] = hi

        def tile(t, _):
            rows = pl.ds(pl.multiple_of(t * 256, 256), 256)
            d = jnp.dot(acat[rows, :], bcat[...], preferred_element_type=F32)
            total = d if first else o_ref[rows, :] + d
            o_ref[rows, :] = total
            return 0

        lax.fori_loop(0, 2, tile, 0)

    a_in = pltpu.make_async_copy(a_ref, abuf.at[q, y, zl], local_sem.at[0])
    a_in.start()
    b_in = pltpu.make_async_copy(b_cols(y), bbuf.at[zh, y, x], local_sem.at[1])
    b_in.start()
    barrier = pltpu.get_barrier_semaphore()
    near = [right_x, left_x, over_z, up_z, down_z, partner] + y_to
    for to in near:
        pl.semaphore_signal(barrier, inc=1, device_id=to, device_id_type=MESH)
    pl.semaphore_wait(barrier, len(near))

    b_spread(zh, y, b_cols(y), True)
    for n, d in enumerate((1, -1, 2)):
        go(remote(b_cols(at_y(d)), bbuf.at[zh, y, x], y_send.at[n], b_recv.at[zh, y, x, 0], y_to[n]))
    a_slot(0)
    a_in.wait()
    b_in.wait()

    oh = 1 - zh
    b_own(1, zh, True)
    b_own(2, zh, True)
    a_slot(1)
    a_slot(2)
    b_relay(0, zh)
    b_own(3, zh, True)
    a_slot(3)
    a_slot(4)
    b_relay(1, zh)
    a_slot(5)
    a_slot(6)
    b_relay(2, zh)
    a_from_y(0)
    b_own(0, oh, False)
    a_from_y(1)
    a_from_y(2)
    b_relay(3, zh)
    a_from_y(3)
    a_from_y(4)
    a_from_y(5)
    a_from_y(6)
    b_own(1, oh, False)
    b_relay(0, oh)

    def b_far(k, h):
        b_wait(h, at_y(STEPS[k]), at_x(2), 0)
        b_wait(h, at_y(STEPS[k]), at_x(2), 1)

    for k in range(4):
        a_partner(at_y(STEPS[k]))
    b_far(0, zh)
    compute(0, zh, first=True)
    b_far(1, zh)
    compute(1, zh)
    b_own(2, oh, False)
    b_relay(1, oh)
    b_far(2, zh)
    compute(2, zh)
    b_far(3, zh)
    compute(3, zh)
    b_own(3, oh, False)
    b_relay(2, oh)
    b_far(0, oh)
    compute(0, oh)
    b_far(1, oh)
    compute(1, oh)
    b_relay(3, oh)
    b_far(2, oh)
    compute(2, oh)
    b_far(3, oh)
    compute(3, oh)
    for copy, cond in sent:
        if cond is None:
            copy.wait_send()
        else:
            pl.when(cond)(copy.wait_send)


def shards(amplitudes, integrals):
    dma = pltpu.SemaphoreType.DMA
    product = pl.pallas_call(
        kernel,
        out_shape=jax.ShapeDtypeStruct((512, 512), F32),
        in_specs=[pl.BlockSpec(memory_space=pltpu.MemorySpace.HBM)] * 2,
        out_specs=pl.BlockSpec(memory_space=pltpu.VMEM),
        scratch_shapes=[
            pltpu.VMEM((2, 4, 4, 64, 512), F32),
            pltpu.VMEM((2, 4, 4, 64, 512), F32),
            pltpu.VMEM((512, 768), BF16),
            pltpu.VMEM((768, 512), BF16),
            dma((2,)),
            dma((2, 4, 4)),
            dma((2, 4, 4, 2)),
            dma((4, 4, 6)),
            dma((2, 4, 3)),
            dma((3,)),
            dma((2, 4, 2)),
        ],
        compiler_params=pltpu.CompilerParams(
            collective_id=0, has_side_effects=True, vmem_limit_bytes=24 * 1024 * 1024
        ),
        name="ladder",
    )(amplitudes.T, integrals)
    return 0.5 * product


def solution(mesh):
    in_specs = (P("row", ("col", "layer")), P(("row", "layer"), "col"))
    out_specs = P("row", ("col", "layer"))
    return jax.shard_map(shards, mesh=mesh, in_specs=in_specs, out_specs=out_specs, check_vma=False)
```

```python
import jax
import jax.numpy as jnp
from jax import lax
from jax.experimental import pallas as pl
from jax.experimental.pallas import tpu as pltpu
from jax.sharding import PartitionSpec as P

MESH = pl.DeviceIdType.MESH
F32, BF16 = jnp.float32, jnp.bfloat16
STEPS = (0, -1, 1, 2)
NEAR, FAR = 1, 2
PIECES = max(NEAR, FAR)


def split(v):
    hi = v.astype(BF16)
    return hi, (v - hi.astype(F32)).astype(BF16)


def kernel(
    a_ref, b_ref, o_ref, abuf, bbuf, acat, bcat,
    local_sem, a_recv, b_recv, a_send, x_send, z_send, y_send, relay_send,
):
    row, col, y = lax.axis_index("row"), lax.axis_index("col"), lax.axis_index("layer")
    x, zh, zl, q = row // 2, row % 2, col // 2, col % 2
    z, oh = zh * 4 + zl, 1 - zh

    def device(x_at, y_at, z_at, q_at):
        x_at, y_at, z_at = (x_at + 4) % 4, (y_at + 4) % 4, (z_at + 8) % 8
        return (x_at * 2 + z_at // 4, (z_at % 4) * 2 + q_at, y_at)

    right_x, left_x = device(x + 1, y, z, q), device(x - 1, y, z, q)
    over_z = device(x, y, z + 4, q)
    up_z, down_z = device(x, y, z + 1, q), device(x, y, z - 1, q)
    partner = device(x, y, z, 1 - q)
    y_to = [device(x, y + d, z, q) for d in (1, -1, 2)]

    def at_y(k):
        return (y + STEPS[k] + 4) % 4

    def at_x(d):
        return (x + d + 4) % 4

    def remote(src, dst, send, recv, to):
        return pltpu.make_async_remote_copy(
            src_ref=src, dst_ref=dst, send_sem=send, recv_sem=recv, device_id=to, device_id_type=MESH
        )

    def wait(dst, sem):
        pltpu.make_async_copy(dst, dst, sem).wait()

    def b_cols(y_at):
        return b_ref.at[:, pl.ds(pl.multiple_of(y_at * 512, 512), 512)]

    sent = []

    def go(copy, cond=None):
        if cond is None:
            copy.start()
        else:
            pl.when(cond)(copy.start)
        sent.append((copy, cond))

    def pieces(h):
        return NEAR if h is zh else FAR

    def b_rows(h, y_at, x_at, p, part=None):
        n = 64 // pieces(h)
        if part is None:
            return bbuf.at[h, y_at, x_at, pl.ds(p * n, n)]
        return bbuf.at[h, y_at, x_at, pl.ds(p * n + part * (n // 2), n // 2)]

    def to_x(k, h, p, src=None):
        y_at = at_y(k)
        dst = b_rows(h, y_at, x, p)
        n = 64 // pieces(h)
        src = dst if src is None else src.at[pl.ds(p * n, n)]
        go(remote(src, dst, x_send.at[h, y_at, p, 0], b_recv.at[h, y_at, x, 2 * p], right_x))
        go(remote(src, dst, x_send.at[h, y_at, p, 1], b_recv.at[h, y_at, x, 2 * p], left_x))

    def to_z(k, p):
        y_at, n = at_y(k), 64 // FAR
        dst = bbuf.at[zh, y_at, x, pl.ds(p * n, n)]
        src = b_cols(y).at[pl.ds(p * n, n)] if k == 0 else dst
        go(remote(src, dst, z_send.at[y_at, p], b_recv.at[zh, y_at, x, 2 * p], over_z))

    def own(k, p):
        wait(b_rows(zh, at_y(k), x, p), b_recv.at[zh, at_y(k), x, 2 * p])
        to_x(k, zh, p)

    def to_y(d, p):
        n = 64 // NEAR
        i = (1, -1, 2).index(d)
        src = b_cols((y + d + 4) % 4).at[pl.ds(p * n, n)]
        go(remote(src, b_rows(zh, y, x, p), y_send.at[i, p], b_recv.at[zh, y, x, 2 * p], y_to[i]))

    def far(k, p):
        wait(b_rows(oh, at_y(k), x, p), b_recv.at[oh, at_y(k), x, 2 * p])
        to_x(k, oh, p)

    def relay(k, h, p=0):
        y_at = at_y(k)
        for part, (d, to) in enumerate(((-1, right_x), (1, left_x))):
            x_at = at_x(d)
            wait(b_rows(h, y_at, x_at, p), b_recv.at[h, y_at, x_at, 2 * p])
            half = b_rows(h, y_at, x_at, p, part)
            go(remote(half, half, relay_send.at[h, y_at, p, part], b_recv.at[h, y_at, x_at, 2 * p + part], to))

    def last(k, h):
        for p in range(pieces(h)):
            for part in range(2):
                wait(b_rows(h, at_y(k), at_x(2), p, part), b_recv.at[h, at_y(k), at_x(2), 2 * p + part])

    def a_wait(q_at, y_at, zl_at):
        wait(abuf.at[q_at, y_at, zl_at], a_recv.at[q_at, y_at, zl_at, 0])

    def a_half(y_at, zl_at, part):
        return abuf.at[q, y_at, zl_at, pl.ds(part * 32, 32)]

    def a_copy(y_at, zl_at, i, to, mine=False):
        blk = abuf.at[q, y_at, zl_at]
        return remote(a_ref if mine else blk, blk, a_send.at[y_at, zl_at, i], a_recv.at[q, y_at, zl_at, 0], to)

    slots = [(0, None, 0)]
    for s in (1, 2, 3):
        slots += [(-s, zl >= s, 1), (s, zl + s <= 3, -1)]

    def both(a, b):
        return b if a is None else jnp.logical_and(a, b)

    def a_along_z(i):
        d, cond, way = slots[i]
        zl_at = jnp.clip(zl + d, 0, 3)
        if way != 0:
            pl.when(cond)(lambda: a_wait(q, y, zl_at))
        if way >= 0:
            go(a_copy(y, zl_at, 0, up_z, way == 0), both(cond, zl <= 2))
        if way <= 0:
            go(a_copy(y, zl_at, 1, down_z, way == 0), both(cond, zl >= 1))

    def a_along_y(i):
        d, cond, way = slots[i]
        zl_at = jnp.clip(zl + d, 0, 3)
        for n in range(2):
            go(a_copy(y, zl_at, 2 + n, y_to[n], way == 0), cond)
        go(a_copy(y, zl_at, 5, partner, way == 0), cond)

    def a_slot(i):
        a_along_z(i)
        a_along_y(i)

    def a_from_y(i):
        d, cond, _ = slots[i]
        zl_at = jnp.clip(zl + d, 0, 3)

        def arrived(y_at):
            a_wait(q, y_at, zl_at)

        for part, k in enumerate((1, 2)):
            y_at = at_y(k)
            if cond is None:
                arrived(y_at)
            else:
                pl.when(cond)(lambda: arrived(y_at))
            half = a_half(y_at, zl_at, part)
            go(remote(half, half, a_send.at[y_at, zl_at, 4], a_recv.at[q, y_at, zl_at, part], y_to[part]), cond)
            go(a_copy(y_at, zl_at, 5, partner), cond)

    def a_far_y(i):
        d, cond, _ = slots[i]
        zl_at = jnp.clip(zl + d, 0, 3)
        y_at = at_y(3)

        def arrived():
            for part in range(2):
                wait(a_half(y_at, zl_at, part), a_recv.at[q, y_at, zl_at, part])

        if cond is None:
            arrived()
        else:
            pl.when(cond)(arrived)
        go(a_copy(y_at, zl_at, 5, partner), cond)

    def a_partner(k):
        for zl_at in range(4):
            a_wait(1 - q, at_y(k), zl_at)

    def a_ready(k, h):
        y_at = at_y(k)
        for p in range(2):
            for rows in range(0, 512, 128):
                v = jnp.concatenate(
                    [abuf[h, y_at, i, p * 32:p * 32 + 32, rows:rows + 128] for i in range(4)], axis=0
                )
                hi, lo = split(v.T)
                acat[p, rows:rows + 128, 0:128] = hi
                acat[p, rows:rows + 128, 128:256] = hi
                acat[p, rows:rows + 128, 256:384] = lo

    def b_ready(k, h, p):
        y_at = at_y(k)
        for i in range(4):
            hi, lo = split(bbuf[h, y_at, i, p * 32:p * 32 + 32, :])
            bcat[p, i * 32:i * 32 + 32] = hi
            bcat[p, 128 + i * 32:128 + i * 32 + 32] = lo
            bcat[p, 256 + i * 32:256 + i * 32 + 32] = hi

    def multiply(groups, first=False):
        def tile(t, _):
            rows = pl.ds(pl.multiple_of(t * 256, 256), 256)
            lhs = jnp.concatenate([acat[p, rows, :] for p in groups], axis=1)
            rhs = jnp.concatenate([bcat[p] for p in groups], axis=0)
            d = jnp.dot(lhs, rhs, preferred_element_type=F32)
            o_ref[rows, :] = d if first else o_ref[rows, :] + d
            return 0

        lax.fori_loop(0, 2, tile, 0)

    def compute(k, h, first=False):
        last(k, h)
        a_ready(k, h)
        b_ready(k, h, 0)
        b_ready(k, h, 1)
        multiply((0, 1), first)

    def last_piece(k, h, p):
        for part in range(2):
            wait(b_rows(h, at_y(k), at_x(2), p, part), b_recv.at[h, at_y(k), at_x(2), 2 * p + part])

    a_in = pltpu.make_async_copy(a_ref, abuf.at[q, y, zl], local_sem.at[0])
    a_in.start()
    b_in = pltpu.make_async_copy(b_cols(y), bbuf.at[zh, y, x], local_sem.at[1])
    b_in.start()
    barrier = pltpu.get_barrier_semaphore()
    near = [over_z, right_x, left_x, up_z, down_z, partner] + y_to
    for to in near:
        pl.semaphore_signal(barrier, inc=1, device_id=to, device_id_type=MESH)
    a_in.wait()
    b_in.wait()
    pl.semaphore_wait(barrier, len(near))

    for p in range(NEAR):
        to_x(0, zh, p, b_cols(y))
    for p in range(NEAR):
        to_y(1, p)
        to_y(-1, p)
    a_along_z(0)
    to_z(0, 0)
    for p in range(NEAR):
        to_y(2, p)
    a_along_y(0)
    to_z(0, 1)
    relay(0, zh, 0)
    own(1, 0)
    to_z(1, 0)
    to_z(1, 1)
    own(2, 0)
    to_z(2, 0)
    to_z(2, 1)
    a_along_z(1)
    a_along_y(1)
    a_along_z(2)
    a_along_y(2)
    own(3, 0)
    to_z(3, 0)
    to_z(3, 1)
    relay(1, zh, 0)
    far(0, 0)
    relay(2, zh, 0)
    far(0, 1)
    a_from_y(0)
    relay(3, zh, 0)
    far(1, 0)
    a_from_y(1)
    relay(0, oh, 0)
    far(1, 1)
    a_from_y(2)
    a_far_y(0)
    relay(0, oh, 1)
    far(2, 0)
    a_far_y(1)
    relay(1, oh, 0)
    far(2, 1)
    relay(1, oh, 1)
    a_far_y(2)
    a_along_z(3)
    a_along_y(3)
    a_along_z(4)
    a_along_y(4)
    relay(2, oh, 0)
    far(3, 0)
    relay(2, oh, 1)
    far(3, 1)
    a_along_z(5)
    a_along_y(5)
    a_along_z(6)
    a_along_y(6)
    relay(3, oh, 0)
    a_from_y(3)
    a_from_y(4)
    a_partner(0)
    compute(0, zh, True)
    compute(0, oh)
    relay(3, oh, 1)
    a_from_y(5)
    a_from_y(6)
    a_partner(1)
    compute(1, zh)
    a_partner(2)
    compute(2, zh)
    compute(1, oh)
    compute(2, oh)
    a_far_y(3)
    a_far_y(4)
    a_far_y(5)
    a_far_y(6)
    a_partner(3)
    compute(3, zh)
    a_ready(3, oh)
    for g in range(2):
        for p in range(g * FAR // 2, (g + 1) * FAR // 2):
            last_piece(3, oh, p)
        b_ready(3, oh, g)
        multiply((g,))

    for copy, cond in sent:
        if cond is None:
            copy.wait_send()
        else:
            pl.when(cond)(copy.wait_send)


def shards(amplitudes, integrals):
    dma = pltpu.SemaphoreType.DMA
    hbm = pltpu.MemorySpace.HBM
    product = pl.pallas_call(
        kernel,
        out_shape=pltpu.VMEM((512, 512), F32),
        in_specs=[pl.BlockSpec(memory_space=hbm)] * 2,
        out_specs=pl.BlockSpec(memory_space=pltpu.VMEM),
        scratch_shapes=[
            pltpu.VMEM((2, 4, 4, 64, 512), F32),
            pltpu.VMEM((2, 4, 4, 64, 512), F32),
            pltpu.VMEM((2, 512, 384), BF16),
            pltpu.VMEM((2, 384, 512), BF16),
            dma((2,)),
            dma((2, 4, 4, 2)),
            dma((2, 4, 4, 2 * PIECES)),
            dma((4, 4, 6)),
            dma((2, 4, PIECES, 2)),
            dma((4, PIECES)),
            dma((3, NEAR)),
            dma((2, 4, PIECES, 2)),
        ],
        compiler_params=pltpu.CompilerParams(
            collective_id=0, has_side_effects=True, vmem_limit_bytes=40 * 1024 * 1024
        ),
        name="ladder",
    )(
        pltpu.with_memory_space_constraint(amplitudes.T, hbm),
        pltpu.with_memory_space_constraint(integrals, hbm),
    )
    return 0.5 * product


def solution(mesh):
    in_specs = (P("row", ("col", "layer")), P(("row", "layer"), "col"))
    out_specs = P("row", ("col", "layer"))
    return jax.shard_map(shards, mesh=mesh, in_specs=in_specs, out_specs=out_specs, check_vma=False)
```
